128 devices in a mesh: dp: 2 (over core), expert: 64 (over y, x, z).
Axes of the slice: x: 4, y: 4, z: 4, core: 2. Of those that a mesh axis runs over, the one named last changes fastest.
Arguments:
- tokens: bfloat16 [16384, 2048], P(('dp', 'expert')), may hold values from -6 to 6
- expert_ids: int32 [16384, 4], P(('dp', 'expert')), may hold values from 0 to 63, all different within a row; in each aligned block of 128 rows (0 to 127, 128 to 255, ...) at most 12 rows name the same one
- gate_weights: float32 [16384, 4], P(('dp', 'expert')), may hold values from 0.2 to 1
- w_gate: bfloat16 [64, 2048, 768], P('expert'), may hold values from -0.125 to 0.125
- w_up: bfloat16 [64, 2048, 768], P('expert'), may hold values from -0.125 to 0.125
- w_down: bfloat16 [64, 768, 2048], P('expert'), may hold values from -0.21875 to 0.21875
- out_grad: bfloat16 [16384, 2048], P(('dp', 'expert')), may hold values from -6 to 6
Outputs:
- mixed: bfloat16 [16384, 2048], P(('dp', 'expert'))
- grad_tokens: bfloat16 [16384, 2048], P(('dp', 'expert'))
- grad_gate: bfloat16 [64, 2048, 768], P('expert')
- grad_up: bfloat16 [64, 2048, 768], P('expert')
- grad_down: bfloat16 [64, 768, 2048], P('expert')
The draws below stay inside these ranges and needn't reach their ends.
Inputs may be any that keep to these rules, and one draw needn't show every extreme that they name: `expert_ids`: each row names 4 different experts. Within the 128 rows of one device no expert is named by more than 12 rows, and in every draw some expert is named by exactly 12 rows of some device.
All inputs are finite; a program needn't handle non-finite values.
Results may differ from the reference program's by a relative error of at most 0.0066.
Values may be sent and summed in bfloat16 or wider, within the bound.
No kernel may reach another device: no remote copies, remote signals or barrier semaphores. Data moves between devices by JAX's collectives and lax.ppermute only.
A program may use at most 128 MiB of HBM per device.

```python
import math
import jax
import jax.numpy as jnp
import numpy as np
from jax import lax

D = 2048
FF = 768
TOP = 4
TOK_DEV = 128
EXPERTS = 64
MOST = 12
TOKENS = 16384
N_DP = 2
N_EXPERT = 64


def block_levels(stream_key, shape, pieces, smallest, high):
    factor_of = 1.0
    for dim, shards_of in pieces:
        steps = jax.random.uniform(jax.random.fold_in(jax.random.fold_in(stream_key, 6), dim), (shards_of,), jnp.float32, smallest / len(pieces), high / len(pieces))
        factor_of = factor_of * jnp.repeat(jnp.exp(steps), shape[dim] // shards_of).reshape((-1,) + (1,) * (len(shape) - 1 - dim))
    return factor_of


def assign_block(stream_key, own, number, rows, amount, top, reach, lean):
    ranking = jax.random.permutation(stream_key, amount)
    crowded, usual = shares(amount, rows * top, reach, lean, True), shares(amount, rows * top, reach, lean, False)
    places = jnp.arange(amount)

    def named(tallies, rotation):
        used = int((tallies > 0).sum())
        fixed = max(1, used // 4)
        moved = fixed + (places - fixed + rotation * (used - fixed)) % max(1, amount - fixed)
        return jnp.zeros((amount,), jnp.int32).at[ranking[jnp.where(places < fixed, places, moved)]].set(jnp.asarray(tallies, jnp.int32))

    tallies = jnp.where(number % 4 == 0, named(crowded, number // 4), named(usual, number - number // 4 - 1))
    mixed = jax.random.permutation(jax.random.fold_in(own, 3), amount)
    source_of, taker = mixed[0:amount // 2 * 2:2], mixed[1:amount // 2 * 2:2]
    room = jnp.minimum(tallies[source_of] - 1, reach - tallies[taker]) // 2
    room = jnp.where((source_of == ranking[0]) | (taker == ranking[0]) | (tallies[taker] == 0), 0, jnp.maximum(room, 0))
    moved = jax.random.randint(jax.random.fold_in(own, 4), (amount // 2,), 0, 1 << 20) % (room + 1)
    tallies = tallies.at[source_of].add(-moved).at[taker].add(moved)
    labels = jnp.searchsorted(jnp.cumsum(tallies), jnp.arange(rows * top), side="right").astype(jnp.int32)
    grid = labels.reshape(top, rows).T
    grid = grid[jax.random.permutation(jax.random.fold_in(own, 1), rows)]
    rotation = jax.random.randint(jax.random.fold_in(own, 2), (rows, 1), 0, top)
    return jnp.take_along_axis(grid, (jnp.arange(top)[None, :] + rotation) % top, axis=1)


def shares(amount, total, limit, lean, full):
    loads = [(1 << 20) // math.isqrt(grade ** lean) + 1 for grade in range(1, amount + 1)]
    largest = limit if full else min(limit, max(-(-total // amount), total * loads[0] // sum(loads)))
    least = 1 if total - largest >= amount - 1 else 0
    holding, spare = [largest] + [least] * (amount - 1), total - largest - least * (amount - 1)
    while spare > 0:
        free = [i for i in range(1, amount) if holding[i] < largest] or [i for i in range(1, amount) if holding[i] < limit]
        mass, budget = sum([loads[i] for i in free]), spare
        for i in free:
            addition = min(limit - holding[i], max(1, budget * loads[i] // mass), spare)
            holding[i] = holding[i] + addition
            spare = spare - addition
    return np.array(holding)


def bell_draw(key, extent, scale, reach, shards=(), kind=jnp.bfloat16):
    gain = block_levels(key, extent, shards, -0.22, 0.18) if shards else 1.0
    drawn = jax.random.normal(key, extent, jnp.float32) * scale * gain
    return jnp.minimum(jnp.maximum(drawn, -reach), reach).astype(kind)


def setup_inputs(seed: int = 0) -> dict:
    key_of = jax.random.split(jax.random.key(seed), 8)
    tokens = bell_draw(key_of[0], (TOKENS, D), 1.0, 6.0, ((0, 128),))
    expert_ids_keys = jax.random.split(jax.random.fold_in(key_of[1], 1), TOKENS // TOK_DEV)
    expert_ids_turns = jax.random.permutation(jax.random.fold_in(key_of[1], 3), TOKENS // TOK_DEV)
    expert_ids = jax.vmap(lambda own, number: assign_block(jax.random.fold_in(key_of[1], 2), own, number, TOK_DEV, EXPERTS, TOP, MOST, 2))(expert_ids_keys, expert_ids_turns).reshape((TOKENS, TOP))
    gate_weights = jnp.clip(0.2 + 0.8 * jax.random.uniform(key_of[2], (TOKENS, TOP), jnp.float32) ** block_levels(key_of[2], (TOKENS, TOP), ((0, 128),), -0.2, 0.2), 0.2, 1.0)
    w_gate = bell_draw(key_of[3], (EXPERTS, D, FF), D ** -0.5, 0.125, ((0, 64),))
    w_up = bell_draw(key_of[4], (EXPERTS, D, FF), D ** -0.5, 0.125, ((0, 64),))
    w_down = bell_draw(key_of[5], (EXPERTS, FF, D), FF ** -0.5, 0.21875, ((0, 64),))
    out_grad = bell_draw(key_of[6], (TOKENS, D), 1.0, 6.0, ((0, 128),))
    return dict(tokens=tokens, expert_ids=expert_ids, gate_weights=gate_weights, w_gate=w_gate, w_up=w_up, w_down=w_down, out_grad=out_grad)


def contract_rows(left, right):
    return lax.dot_general(left, right, (((1,), (1,)), ((), ())), preferred_element_type=jnp.float32)


def contract_cols(left, right):
    return lax.dot_general(left, right, (((0,), (0,)), ((), ())), preferred_element_type=jnp.float32)


def forward_rows(row_block, w_first, w_second, w_third):
    pre_gate = jnp.dot(row_block, w_first, preferred_element_type=jnp.float32)
    pre_up = jnp.dot(row_block, w_second, preferred_element_type=jnp.float32)
    hidden = (pre_gate * jax.nn.sigmoid(pre_gate) * pre_up).astype(jnp.bfloat16)
    result = jnp.dot(hidden, w_third, preferred_element_type=jnp.float32).astype(jnp.bfloat16)
    return pre_gate, pre_up, hidden, result


def backward_rows(cotangent, pre_gate, pre_up, w_first, w_second, w_third):
    d_hidden = contract_rows(cotangent, w_third)
    sig_gate = jax.nn.sigmoid(pre_gate)
    d_gate = (d_hidden * pre_up * sig_gate * (1.0 + pre_gate * (1.0 - sig_gate))).astype(jnp.bfloat16)
    d_up = (d_hidden * pre_gate * sig_gate).astype(jnp.bfloat16)
    d_rows = (contract_rows(d_gate, w_first) + contract_rows(d_up, w_second)).astype(jnp.bfloat16)
    return d_gate, d_up, d_rows


def reference(tokens, expert_ids, gate_weights, w_gate, w_up, w_down, out_grad):
    replica_rows = TOKENS // N_DP
    capacity = N_EXPERT * MOST
    model_width = tokens.shape[1]

    def per_expert(carried, expert):
        mixed_acc, grad_acc = carried
        partials = []
        for replica in range(N_DP):
            block_ids = expert_ids[replica * replica_rows:(replica + 1) * replica_rows].reshape(-1)
            hits = block_ids == expert
            found = jnp.nonzero(hits, size=capacity, fill_value=0)[0].astype(jnp.int32)
            is_live = jnp.arange(capacity, dtype=jnp.int32) < jnp.sum(hits.astype(jnp.int32))
            token_pos = found // TOP + replica * replica_rows
            pick_pos = found % TOP
            gate_val = jnp.where(is_live, gate_weights[token_pos, pick_pos], jnp.zeros((), gate_weights.dtype))
            row_block = jnp.where(is_live[:, None], tokens[token_pos], jnp.zeros((), tokens.dtype))
            w_first = w_gate[expert]
            w_second = w_up[expert]
            w_third = w_down[expert]
            pre_gate, pre_up, hidden, result = forward_rows(row_block, w_first, w_second, w_third)
            mixed_acc = mixed_acc.at[token_pos].add(gate_val[:, None] * result.astype(jnp.float32))
            cotangent = (gate_val[:, None] * out_grad[token_pos].astype(jnp.float32)).astype(jnp.bfloat16)
            d_gate, d_up, d_rows = backward_rows(cotangent, pre_gate, pre_up, w_first, w_second, w_third)
            grad_acc = grad_acc.at[token_pos].add(jnp.where(is_live[:, None], d_rows.astype(jnp.float32), jnp.zeros((), jnp.float32)))
            part_gate = contract_cols(row_block, d_gate).astype(jnp.bfloat16)
            part_up = contract_cols(row_block, d_up).astype(jnp.bfloat16)
            part_down = contract_cols(hidden, cotangent).astype(jnp.bfloat16)
            partials.append((part_gate, part_up, part_down))
        sum_gate = partials[0][0].astype(jnp.float32)
        sum_up = partials[0][1].astype(jnp.float32)
        sum_down = partials[0][2].astype(jnp.float32)
        for replica in range(1, N_DP):
            sum_gate = sum_gate + partials[replica][0].astype(jnp.float32)
            sum_up = sum_up + partials[replica][1].astype(jnp.float32)
            sum_down = sum_down + partials[replica][2].astype(jnp.float32)
        totals = (sum_gate.astype(jnp.bfloat16), sum_up.astype(jnp.bfloat16), sum_down.astype(jnp.bfloat16))
        return (mixed_acc, grad_acc), totals

    start_acc = (jnp.zeros((TOKENS, model_width), jnp.float32), jnp.zeros((TOKENS, model_width), jnp.float32))
    finals, grads = lax.scan(per_expert, start_acc, jnp.arange(EXPERTS, dtype=jnp.int32))
    mixed = finals[0].astype(jnp.bfloat16)
    grad_tokens = finals[1].astype(jnp.bfloat16)
    return mixed, grad_tokens, grads[0], grads[1], grads[2]
```

```python
import jax
import jax.numpy as jnp
from jax import lax
from jax.experimental import pallas as pl
from jax.experimental.pallas import tpu as pltpu
from jax.sharding import PartitionSpec as P

F32 = jnp.float32
BF16 = jnp.bfloat16
FULL = 8
PART = 4
NO_SLOT = 99.0


def dot(left, right):
    return jnp.dot(left, right, preferred_element_type=F32)


def contract_rows(left, right):
    return lax.dot_general(left, right, (((1,), (1,)), ((), ())), preferred_element_type=F32)


def contract_cols(left, right):
    return lax.dot_general(left, right, (((0,), (0,)), ((), ())), preferred_element_type=F32)


def iota(shape, dim):
    return lax.broadcasted_iota(jnp.int32, shape, dim)


def dispatch_body(experts, ids_ref, gates_ref, tokens_ref, grad_ref, first_ref, second_ref, both_ref, sems):
    rows = tokens_ref.shape[0]

    @pl.when(pl.program_id(0) == 0)
    def _():
        copies = [
            pltpu.make_async_copy(tokens_ref, both_ref.at[pl.ds(0, rows)], sems.at[0]),
            pltpu.make_async_copy(grad_ref, both_ref.at[pl.ds(rows, rows)], sems.at[1]),
        ]
        for copy in copies:
            copy.start()
        for copy in copies:
            copy.wait()

    expert = iota((experts, rows), 0) + pl.program_id(0) * experts
    member = jnp.zeros((experts, rows), F32)
    gate = jnp.zeros((experts, rows), F32)
    for k in range(ids_ref.shape[0]):
        hit = ids_ref[k : k + 1, :] == expert
        member = jnp.where(hit, 1.0, member)
        gate = jnp.where(hit, gates_ref[k : k + 1, :], gate)
    earlier = jnp.where(iota((rows, rows), 0) < iota((rows, rows), 1), 1.0, 0.0).astype(BF16)
    rank = jnp.where(member > 0.5, dot(member.astype(BF16), earlier), NO_SLOT)

    def fill(out_ref, depth, base):
        shape = (experts, 2 * depth, rows)
        flat = (experts * 2 * depth, rows)
        row = iota(shape, 1)
        slot = (jnp.where(row < depth, row, row - depth) + base).astype(F32)
        is_token = row < depth
        hit = rank[:, None, :] == slot
        one = jnp.where(hit, 1.0, 0.0)
        of_token = jnp.where(is_token, one, 0.0).reshape(flat)
        of_grad = jnp.where(is_token, 0.0, one).reshape(flat)
        scale = jnp.where(hit, jnp.broadcast_to(gate[:, None, :], shape), 0.0)
        scale = jnp.sum(jnp.where(is_token, one, scale).reshape(flat), axis=1, keepdims=True)
        pick = jnp.concatenate([of_token, of_grad], axis=1).astype(BF16)
        out_ref[...] = (dot(pick, both_ref[...]) * scale).astype(BF16)

    fill(first_ref, FULL, 0)
    fill(second_ref, PART, FULL)


def dispatch(ids_t, gates_t, tokens, out_grad, experts, per_step):
    rows, width = tokens.shape
    top = ids_t.shape[0]
    whole = lambda shape: pl.BlockSpec(shape, lambda i: (0, 0))
    return pl.pallas_call(
        lambda *refs: dispatch_body(per_step, *refs),
        grid=(experts // per_step,),
        in_specs=[
            whole((top, rows)),
            whole((top, rows)),
            pl.BlockSpec(memory_space=pl.ANY),
            pl.BlockSpec(memory_space=pl.ANY),
        ],
        out_specs=[
            pl.BlockSpec((per_step * 2 * FULL, width), lambda i: (i, 0)),
            pl.BlockSpec((per_step * 2 * PART, width), lambda i: (i, 0)),
        ],
        out_shape=[
            jax.ShapeDtypeStruct((experts * 2 * FULL, width), BF16),
            jax.ShapeDtypeStruct((experts * 2 * PART, width), BF16),
        ],
        scratch_shapes=[pltpu.VMEM((2 * rows, width), BF16), pltpu.SemaphoreType.DMA((2,))],
        name="dispatch",
    )(ids_t, gates_t, tokens, out_grad)


def picker_body(experts, depth, ids_ref, gates_ref, pick_ref):
    rows, top = ids_ref.shape
    expert = iota((rows, experts), 1)
    member = jnp.zeros((rows, experts), F32)
    gate = jnp.zeros((rows, experts), F32)
    for k in range(top):
        hit = ids_ref[:, k : k + 1] == expert
        member = jnp.where(hit, 1.0, member)
        gate = jnp.where(hit, gates_ref[:, k : k + 1], gate)
    later = jnp.where(iota((rows, rows), 1) < iota((rows, rows), 0), 1.0, 0.0).astype(BF16)
    rank = jnp.where(member > 0.5, dot(later, member.astype(BF16)), NO_SLOT)
    high = gate.astype(BF16)
    low = (gate - high.astype(F32)).astype(BF16)
    total = experts * 2 * depth
    lane = iota((experts, total), 1) // (2 * depth)
    spread = jnp.where(lane == iota((experts, total), 0), 1.0, 0.0).astype(BF16)
    place = iota((rows, total), 1) % (2 * depth)
    slot = jnp.where(place < depth, place, jnp.where(place < FULL + 2 * PART, place - PART, place - FULL - 2 * PART))
    hit = dot(rank.astype(BF16), spread) == slot.astype(F32)
    back = hit & (place < depth)
    pick_ref[0:rows, :] = jnp.where(back, dot(high, spread), 0.0).astype(BF16)
    pick_ref[rows : 2 * rows, :] = jnp.where(back, dot(low, spread), 0.0).astype(BF16)
    pick_ref[2 * rows : 3 * rows, :] = jnp.where(hit & (place >= depth), 1.0, 0.0).astype(BF16)


def picker(ids, gates, experts):
    rows = ids.shape[0]
    depth = FULL + PART
    return pl.pallas_call(
        lambda *refs: picker_body(experts, depth, *refs),
        out_shape=jax.ShapeDtypeStruct((3 * rows, experts * 2 * depth), BF16),
        name="picker",
    )(ids, gates)


def combine_body(pick_ref, back_ref, mixed_ref, grad_ref):
    rows = mixed_ref.shape[0]
    total = dot(pick_ref[...], back_ref[...])
    mixed_ref[...] = (total[0:rows] + total[rows : 2 * rows]).astype(BF16)
    grad_ref[...] = total[2 * rows : 3 * rows].astype(BF16)


def combine(pick, back, rows, cols):
    total, width = back.shape
    out = jax.ShapeDtypeStruct((rows, width), BF16)
    return pl.pallas_call(
        combine_body,
        grid=(width // cols,),
        in_specs=[
            pl.BlockSpec((3 * rows, total), lambda i: (0, 0)),
            pl.BlockSpec((total, cols), lambda i: (0, i)),
        ],
        out_specs=[pl.BlockSpec((rows, cols), lambda i: (0, i))] * 2,
        out_shape=[out, out],
        name="combine",
    )(pick, back)


def expert_rows(x, cot, wg_ref, wu_ref, wd_ref):
    pre_gate = dot(x, wg_ref[...])
    pre_up = dot(x, wu_ref[...])
    sig = jax.nn.sigmoid(pre_gate)
    hidden = (pre_gate * sig * pre_up).astype(BF16)
    result = dot(hidden, wd_ref[...]).astype(BF16)
    d_hidden = contract_rows(cot, wd_ref[...])
    d_gate = (d_hidden * pre_up * sig * (1.0 + pre_gate * (1.0 - sig))).astype(BF16)
    d_up = (d_hidden * pre_gate * sig).astype(BF16)
    d_rows = (contract_rows(d_gate, wg_ref[...]) + contract_rows(d_up, wu_ref[...])).astype(BF16)
    return hidden, result, d_gate, d_up, d_rows


def main_body(tok_ref, cot_ref, wg_ref, wu_ref, wd_ref, back_ref, hid_ref, dg_ref, du_ref, res_buf, row_buf, sems):
    group, depth, width = tok_ref.shape
    step = pl.program_id(0)
    slot = step % 2

    def copies(at, buf):
        rows = pl.ds(at * group, group)
        return (
            pltpu.make_async_copy(res_buf.at[buf], back_ref.at[rows, pl.ds(0, FULL)], sems.at[0, buf]),
            pltpu.make_async_copy(row_buf.at[buf], back_ref.at[rows, pl.ds(FULL + 2 * PART, FULL)], sems.at[1, buf]),
        )

    @pl.when(step >= 2)
    def _():
        for copy in copies(step - 2, slot):
            copy.wait()

    flat = (group * depth, width)
    hidden, result, d_gate, d_up, d_rows = expert_rows(
        tok_ref[...].reshape(flat), cot_ref[...].reshape(flat), wg_ref, wu_ref, wd_ref
    )
    hid_ref[...] = hidden
    dg_ref[...] = d_gate
    du_ref[...] = d_up
    res_buf[slot] = result.reshape(group, depth, width)
    row_buf[slot] = d_rows.reshape(group, depth, width)
    for copy in copies(step, slot):
        copy.start()

    @pl.when(step == pl.num_programs(0) - 1)
    def _():
        @pl.when(step >= 1)
        def _():
            for copy in copies(step - 1, 1 - slot):
                copy.wait()

        for copy in copies(step, slot):
            copy.wait()


def main_experts(first, wg, wu, wd, group):
    sources, _, width = first.shape
    hidden_width = wg.shape[1]
    rows = sources * FULL
    small = jax.ShapeDtypeStruct((rows, hidden_width), BF16)
    fixed = lambda w: pl.BlockSpec(w.shape, lambda i: (0, 0), pipeline_mode=pl.Buffered(1))
    return pl.pallas_call(
        main_body,
        grid=(sources // group,),
        in_specs=[
            pl.BlockSpec((group, FULL, width), lambda i: (i, 0, 0)),
            pl.BlockSpec((group, FULL, width), lambda i: (i, 1, 0)),
            fixed(wg),
            fixed(wu),
            fixed(wd),
        ],
        out_specs=[pl.BlockSpec(memory_space=pl.ANY)]
        + [pl.BlockSpec((group * FULL, hidden_width), lambda i: (i, 0))] * 3,
        out_shape=[jax.ShapeDtypeStruct((sources, 2 * (FULL + PART), width), BF16), small, small, small],
        scratch_shapes=[
            pltpu.VMEM((2, group, FULL, width), BF16),
            pltpu.VMEM((2, group, FULL, width), BF16),
            pltpu.SemaphoreType.DMA((2, 2)),
        ],
        name="experts_main",
    )(first, first, wg, wu, wd)


def rest_body(mix_ref, wg_ref, wu_ref, wd_ref, old_ref, back_ref, tok_ref, cot_ref, hid_ref, dg_ref, du_ref, buf, sem):
    sources, depth, width = mix_ref.shape
    block = 256
    half = block // 2
    row = iota((block, block), 0)
    col = iota((block, block), 1)
    local = jnp.where(row < half, row, row - half)
    start = (local // PART) * (2 * PART) + local % PART + jnp.where(row < half, 0, PART)
    apart = jnp.where(col == start, 1.0, 0.0).astype(BF16)
    mix = mix_ref[...].reshape(sources * depth, width)
    n_blocks = sources * depth // block
    toks, cots = [], []
    for b in range(n_blocks):
        parts = dot(apart, mix[b * block : (b + 1) * block]).astype(BF16)
        toks.append(parts[:half])
        cots.append(parts[half:])
    tok = jnp.concatenate(toks, axis=0)
    cot = jnp.concatenate(cots, axis=0)
    hidden, result, d_gate, d_up, d_rows = expert_rows(tok, cot, wg_ref, wu_ref, wd_ref)
    for b in range(n_blocks):
        both = jnp.concatenate([result[b * half : (b + 1) * half], d_rows[b * half : (b + 1) * half]], axis=0)
        part = contract_cols(apart, both).astype(BF16)
        per = block // depth
        buf[b * per : (b + 1) * per] = part.reshape(per, depth, width)
    copy = pltpu.make_async_copy(buf, back_ref.at[:, pl.ds(FULL, 2 * PART)], sem)
    copy.start()
    tok_ref[...] = tok
    cot_ref[...] = cot
    hid_ref[...] = hidden
    dg_ref[...] = d_gate
    du_ref[...] = d_up
    copy.wait()


def rest_experts(second, wg, wu, wd, back):
    sources, depth, width = second.shape
    rows = sources * PART
    hidden_width = wg.shape[1]
    wide = jax.ShapeDtypeStruct((rows, width), BF16)
    small = jax.ShapeDtypeStruct((rows, hidden_width), BF16)
    vmem = pl.BlockSpec(memory_space=pltpu.VMEM)
    return pl.pallas_call(
        rest_body,
        in_specs=[vmem] * 4 + [pl.BlockSpec(memory_space=pl.ANY)],
        out_specs=[pl.BlockSpec(memory_space=pl.ANY)] + [vmem] * 5,
        out_shape=[jax.ShapeDtypeStruct(back.shape, BF16), wide, wide, small, small, small],
        input_output_aliases={4: 0},
        scratch_shapes=[pltpu.VMEM((sources, depth, width), BF16), pltpu.SemaphoreType.DMA(())],
        name="experts_rest",
    )(second, wg, wu, wd, back)


def exchange(blocks):
    return lax.all_to_all(blocks, "expert", split_axis=0, concat_axis=0, tiled=True)


def replica_sum(part):
    other = lax.ppermute(part, "dp", [(0, 1), (1, 0)])
    return (part.astype(F32) + other.astype(F32)).astype(BF16)


def on_device(tokens, expert_ids, gate_weights, w_gate, w_up, w_down, out_grad):
    experts = lax.axis_size("expert")
    rows, width = tokens.shape
    wg, wu, wd = w_gate[0], w_up[0], w_down[0]
    first, second = dispatch(expert_ids.T, gate_weights.T, tokens, out_grad, experts, 8)
    first = exchange(first.reshape(experts, 2 * FULL, width))
    second = exchange(second.reshape(experts, 2 * PART, width))
    pick = picker(expert_ids, gate_weights, experts)
    back, hid_a, dg_a, du_a = main_experts(first, wg, wu, wd, 32)
    back, tok_b, cot_b, hid_b, dg_b, du_b = rest_experts(second, wg, wu, wd, back)
    back = exchange(back).reshape(-1, width)
    tok = jnp.concatenate([first[:, :FULL].reshape(-1, width), tok_b], axis=0)
    cot = jnp.concatenate([first[:, FULL:].reshape(-1, width), cot_b], axis=0)
    hid = jnp.concatenate([hid_a, hid_b], axis=0)
    d_gate = jnp.concatenate([dg_a, dg_b], axis=0)
    d_up = jnp.concatenate([du_a, du_b], axis=0)
    grad_gate = replica_sum(contract_cols(tok, d_gate).astype(BF16))
    grad_up = replica_sum(contract_cols(tok, d_up).astype(BF16))
    grad_down = replica_sum(contract_cols(hid, cot).astype(BF16))
    mixed, grad_tokens = combine(pick, back, rows, 512)
    return mixed, grad_tokens, grad_gate[None], grad_up[None], grad_down[None]


def solution(mesh):
    by_row = P(("dp", "expert"), None)
    by_expert = P("expert", None, None)
    return jax.shard_map(
        on_device,
        mesh=mesh,
        in_specs=(by_row, by_row, by_row, by_expert, by_expert, by_expert, by_row),
        out_specs=(by_row, by_row, by_expert, by_expert, by_expert),
        check_vma=False,
    )
```

```python
import jax
import jax.numpy as jnp
from jax import lax
from jax.experimental import pallas as pl
from jax.experimental.pallas import tpu as pltpu
from jax.sharding import PartitionSpec as P


F32 = jnp.float32
BF16 = jnp.bfloat16
FULL = 8
PART = 4
NO_SLOT = 99.0


def dot(left, right):
    return jnp.dot(left, right, preferred_element_type=F32)


def contract_rows(left, right):
    return lax.dot_general(left, right, (((1,), (1,)), ((), ())), preferred_element_type=F32)


def contract_cols(left, right):
    return lax.dot_general(left, right, (((0,), (0,)), ((), ())), preferred_element_type=F32)


def iota(shape, dim):
    return lax.broadcasted_iota(jnp.int32, shape, dim)


def dispatch_body(experts, ids_ref, gates_ref, tokens_ref, grad_ref, first_ref, second_ref, both_ref, sems):
    rows = tokens_ref.shape[0]

    @pl.when(pl.program_id(0) == 0)
    def _():
        copies = [
            pltpu.make_async_copy(tokens_ref, both_ref.at[pl.ds(0, rows)], sems.at[0]),
            pltpu.make_async_copy(grad_ref, both_ref.at[pl.ds(rows, rows)], sems.at[1]),
        ]
        for copy in copies:
            copy.start()
        for copy in copies:
            copy.wait()

    expert = iota((experts, rows), 0) + pl.program_id(0) * experts
    member = jnp.zeros((experts, rows), F32)
    gate = jnp.zeros((experts, rows), F32)
    for k in range(ids_ref.shape[0]):
        hit = ids_ref[k : k + 1, :] == expert
        member = jnp.where(hit, 1.0, member)
        gate = jnp.where(hit, gates_ref[k : k + 1, :], gate)
    earlier = jnp.where(iota((rows, rows), 0) < iota((rows, rows), 1), 1.0, 0.0).astype(BF16)
    rank = jnp.where(member > 0.5, dot(member.astype(BF16), earlier), NO_SLOT)

    def fill(out_ref, depth, base):
        shape = (experts, 2 * depth, rows)
        flat = (experts * 2 * depth, rows)
        row = iota(shape, 1)
        slot = (jnp.where(row < depth, row, row - depth) + base).astype(F32)
        is_token = row < depth
        hit = rank[:, None, :] == slot
        one = jnp.where(hit, 1.0, 0.0)
        of_token = jnp.where(is_token, one, 0.0).reshape(flat)
        of_grad = jnp.where(is_token, 0.0, one).reshape(flat)
        scale = jnp.where(hit, jnp.broadcast_to(gate[:, None, :], shape), 0.0)
        scale = jnp.sum(jnp.where(is_token, one, scale).reshape(flat), axis=1, keepdims=True)
        pick = jnp.concatenate([of_token, of_grad], axis=1).astype(BF16)
        out_ref[...] = (dot(pick, both_ref[...]) * scale).astype(BF16)

    fill(first_ref, FULL, 0)
    fill(second_ref, PART, FULL)


def dispatch(ids_t, gates_t, tokens, out_grad, experts, per_step):
    rows, width = tokens.shape
    top = ids_t.shape[0]
    whole = lambda shape: pl.BlockSpec(shape, lambda i: (0, 0))
    return pl.pallas_call(
        lambda *refs: dispatch_body(per_step, *refs),
        grid=(experts // per_step,),
        in_specs=[
            whole((top, rows)),
            whole((top, rows)),
            pl.BlockSpec(memory_space=pl.ANY),
            pl.BlockSpec(memory_space=pl.ANY),
        ],
        out_specs=[
            pl.BlockSpec((per_step * 2 * FULL, width), lambda i: (i, 0)),
            pl.BlockSpec((per_step * 2 * PART, width), lambda i: (i, 0)),
        ],
        out_shape=[
            jax.ShapeDtypeStruct((experts * 2 * FULL, width), BF16),
            jax.ShapeDtypeStruct((experts * 2 * PART, width), BF16),
        ],
        scratch_shapes=[pltpu.VMEM((2 * rows, width), BF16), pltpu.SemaphoreType.DMA((2,))],
        name="dispatch",
    )(ids_t, gates_t, tokens, out_grad)


def picker_body(experts, ids_ref, gates_ref, full_ref, part_ref):
    rows, top = ids_ref.shape
    expert = iota((rows, experts), 1)
    member = jnp.zeros((rows, experts), F32)
    gate = jnp.zeros((rows, experts), F32)
    for k in range(top):
        hit = ids_ref[:, k : k + 1] == expert
        member = jnp.where(hit, 1.0, member)
        gate = jnp.where(hit, gates_ref[:, k : k + 1], gate)
    later = jnp.where(iota((rows, rows), 1) < iota((rows, rows), 0), 1.0, 0.0).astype(BF16)
    rank = jnp.where(member > 0.5, dot(later, member.astype(BF16)), NO_SLOT).astype(BF16)
    high = gate.astype(BF16)
    low = (gate - high.astype(F32)).astype(BF16)

    def fill(out_ref, depth, base):
        total = experts * 2 * depth
        spread = jnp.where(iota((experts, total), 1) // (2 * depth) == iota((experts, total), 0), 1.0, 0.0).astype(BF16)
        place = iota((rows, total), 1) % (2 * depth)
        slot = jnp.where(place < depth, place, place - depth) + base
        hit = dot(rank, spread) == slot.astype(F32)
        back = hit & (place < depth)
        out_ref[0:rows, :] = jnp.where(back, dot(high, spread), 0.0).astype(BF16)
        out_ref[rows : 2 * rows, :] = jnp.where(back, dot(low, spread), 0.0).astype(BF16)
        out_ref[2 * rows : 3 * rows, :] = jnp.where(hit & (place >= depth), 1.0, 0.0).astype(BF16)

    fill(full_ref, FULL, 0)
    fill(part_ref, PART, FULL)


def picker(ids, gates, experts):
    rows = ids.shape[0]
    return pl.pallas_call(
        lambda *refs: picker_body(experts, *refs),
        out_shape=[
            jax.ShapeDtypeStruct((3 * rows, experts * 2 * FULL), BF16),
            jax.ShapeDtypeStruct((3 * rows, experts * 2 * PART), BF16),
        ],
        name="picker",
    )(ids, gates)


def gather_body(pick_ref, back_ref, mixed_ref, grad_ref):
    rows = mixed_ref.shape[0]
    total = dot(pick_ref[...], back_ref[...])
    mixed_ref[...] = total[0:rows] + total[rows : 2 * rows]
    grad_ref[...] = total[2 * rows : 3 * rows]


def finish_body(pick_ref, back_ref, mixed_old_ref, grad_old_ref, mixed_ref, grad_ref):
    rows = mixed_ref.shape[0]
    total = dot(pick_ref[...], back_ref[...])
    mixed_ref[...] = (mixed_old_ref[...] + total[0:rows] + total[rows : 2 * rows]).astype(BF16)
    grad_ref[...] = (grad_old_ref[...] + total[2 * rows : 3 * rows]).astype(BF16)


def gather(pick, back, cols):
    rows = pick.shape[0] // 3
    total, width = back.shape
    out = jax.ShapeDtypeStruct((rows, width), F32)
    by_cols = lambda count: pl.BlockSpec((count, cols), lambda i: (0, i))
    return pl.pallas_call(
        gather_body,
        grid=(width // cols,),
        in_specs=[pl.BlockSpec(pick.shape, lambda i: (0, 0)), by_cols(total)],
        out_specs=[by_cols(rows)] * 2,
        out_shape=[out, out],
        name="gather",
    )(pick, back)


def finish(pick, back, old):
    out = jax.ShapeDtypeStruct(old[0].shape, BF16)
    return pl.pallas_call(
        finish_body,
        in_specs=[pl.BlockSpec(memory_space=pltpu.VMEM)] * 4,
        out_shape=[out, out],
        compiler_params=pltpu.CompilerParams(vmem_limit_bytes=24 << 20),
        name="finish",
    )(*map(in_vmem, (pick, back, *old)))


def in_vmem(array):
    return pltpu.with_memory_space_constraint(array, pltpu.VMEM)


def expert_rows(x, cot, wg_ref, wu_ref, wd_ref):
    pre_gate = dot(x, wg_ref[...])
    pre_up = dot(x, wu_ref[...])
    sig = jax.nn.sigmoid(pre_gate)
    hidden = (pre_gate * sig * pre_up).astype(BF16)
    result = dot(hidden, wd_ref[...]).astype(BF16)
    d_hidden = contract_rows(cot, wd_ref[...])
    d_gate = (d_hidden * pre_up * sig * (1.0 + pre_gate * (1.0 - sig))).astype(BF16)
    d_up = (d_hidden * pre_gate * sig).astype(BF16)
    d_rows = (contract_rows(d_gate, wg_ref[...]) + contract_rows(d_up, wu_ref[...])).astype(BF16)
    return hidden, result, d_gate, d_up, d_rows


def main_body(tok_ref, cot_ref, wg_ref, wu_ref, wd_ref, back_ref, hid_ref, dg_ref, du_ref):
    group, depth, width = tok_ref.shape
    flat = (group * depth, width)
    hidden, result, d_gate, d_up, d_rows = expert_rows(
        tok_ref[...].reshape(flat), cot_ref[...].reshape(flat), wg_ref, wu_ref, wd_ref
    )
    hid_ref[...] = hidden
    dg_ref[...] = d_gate
    du_ref[...] = d_up
    back_ref[:, 0:depth] = result.reshape(group, depth, width)
    back_ref[:, depth : 2 * depth] = d_rows.reshape(group, depth, width)


def main_experts(first, wg, wu, wd, group):
    sources, both, width = first.shape
    hidden_width = wg.shape[1]
    small = jax.ShapeDtypeStruct((sources * FULL, hidden_width), BF16)
    fixed = lambda w: pl.BlockSpec(w.shape, lambda i: (0, 0), pipeline_mode=pl.Buffered(1))
    return pl.pallas_call(
        main_body,
        grid=(sources // group,),
        in_specs=[
            pl.BlockSpec((group, FULL, width), lambda i: (i, 0, 0)),
            pl.BlockSpec((group, FULL, width), lambda i: (i, 1, 0)),
            fixed(wg),
            fixed(wu),
            fixed(wd),
        ],
        out_specs=[pl.BlockSpec((group, both, width), lambda i: (i, 0, 0))]
        + [pl.BlockSpec((group * FULL, hidden_width), lambda i: (i, 0))] * 3,
        out_shape=[jax.ShapeDtypeStruct(first.shape, BF16), small, small, small],
        name="experts_main",
    )(first, first, wg, wu, wd)


def rest_body(mix_ref, wg_ref, wu_ref, wd_ref, back_ref, tok_ref, cot_ref, hid_ref, dg_ref, du_ref):
    sources, depth, width = mix_ref.shape
    block = 256
    half = block // 2
    row = iota((block, block), 0)
    col = iota((block, block), 1)
    local = jnp.where(row < half, row, row - half)
    start = (local // PART) * (2 * PART) + local % PART + jnp.where(row < half, 0, PART)
    apart = jnp.where(col == start, 1.0, 0.0).astype(BF16)
    mix = mix_ref[...].reshape(sources * depth, width)
    n_blocks = sources * depth // block
    toks, cots = [], []
    for b in range(n_blocks):
        parts = dot(apart, mix[b * block : (b + 1) * block]).astype(BF16)
        toks.append(parts[:half])
        cots.append(parts[half:])
    tok = jnp.concatenate(toks, axis=0)
    cot = jnp.concatenate(cots, axis=0)
    hidden, result, d_gate, d_up, d_rows = expert_rows(tok, cot, wg_ref, wu_ref, wd_ref)
    per = block // depth
    for b in range(n_blocks):
        both = jnp.concatenate([result[b * half : (b + 1) * half], d_rows[b * half : (b + 1) * half]], axis=0)
        back_ref[b * per : (b + 1) * per] = contract_cols(apart, both).astype(BF16).reshape(per, depth, width)
    tok_ref[...] = tok
    cot_ref[...] = cot
    hid_ref[...] = hidden
    dg_ref[...] = d_gate
    du_ref[...] = d_up


def rest_experts(second, wg, wu, wd):
    sources, _, width = second.shape
    rows = sources * PART
    wide = jax.ShapeDtypeStruct((rows, width), BF16)
    small = jax.ShapeDtypeStruct((rows, wg.shape[1]), BF16)
    return pl.pallas_call(
        rest_body,
        in_specs=[pl.BlockSpec(memory_space=pltpu.VMEM)] * 4,
        out_shape=[jax.ShapeDtypeStruct(second.shape, BF16), wide, wide, small, small, small],
        compiler_params=pltpu.CompilerParams(vmem_limit_bytes=48 << 20),
        name="experts_rest",
    )(in_vmem(second), wg, wu, wd)


def exchange(blocks):
    return lax.all_to_all(blocks, "expert", split_axis=0, concat_axis=0, tiled=True)


def replica_sum(part):
    other = lax.ppermute(part, "dp", [(0, 1), (1, 0)])
    return (part.astype(F32) + other.astype(F32)).astype(BF16)


def layer(tokens, expert_ids, gate_weights, w_gate, w_up, w_down, out_grad):
    experts = lax.axis_size("expert")
    _, width = tokens.shape
    wg, wu, wd = w_gate[0], w_up[0], w_down[0]
    first, second = dispatch(expert_ids.T, gate_weights.T, tokens, out_grad, experts, 8)
    first = exchange(first.reshape(experts, 2 * FULL, width))
    first, second = lax.optimization_barrier((first, second))
    second = exchange(second.reshape(experts, 2 * PART, width))
    pick_full, pick_part = picker(expert_ids, gate_weights, experts)
    full, hid_a, dg_a, du_a = main_experts(first, wg, wu, wd, 32)
    part, tok_b, cot_b, hid_b, dg_b, du_b = rest_experts(second, wg, wu, wd)
    full = exchange(full)
    tok = jnp.concatenate([first[:, :FULL].reshape(-1, width), tok_b], axis=0)
    cot = jnp.concatenate([first[:, FULL:].reshape(-1, width), cot_b], axis=0)
    hid = jnp.concatenate([hid_a, hid_b], axis=0)
    d_gate = jnp.concatenate([dg_a, dg_b], axis=0)
    d_up = jnp.concatenate([du_a, du_b], axis=0)
    grad_gate = replica_sum(contract_cols(tok, d_gate).astype(BF16))
    grad_up = replica_sum(contract_cols(tok, d_up).astype(BF16))
    grad_down = replica_sum(contract_cols(hid, cot).astype(BF16))
    full, part, pick_full, pick_part, grad_gate, grad_up = lax.optimization_barrier(
        (full, part, pick_full, pick_part, grad_gate, grad_up)
    )
    full = full.reshape(-1, width)
    part = exchange(part).reshape(-1, width)
    old = gather(pick_full, full, 512)
    mixed, grad_tokens = finish(pick_part, part, old)
    return mixed, grad_tokens, grad_gate[None], grad_up[None], grad_down[None]


def solution(mesh):
    by_row = P(("dp", "expert"), None)
    by_expert = P("expert", None, None)
    return jax.shard_map(
        layer,
        mesh=mesh,
        in_specs=(by_row, by_row, by_row, by_expert, by_expert, by_expert, by_row),
        out_specs=(by_row, by_row, by_expert, by_expert, by_expert),
        check_vma=False,
    )
```

```python
import jax
import jax.numpy as jnp
from jax import lax
from jax.experimental import pallas as pl
from jax.experimental.pallas import tpu as pltpu
from jax.sharding import PartitionSpec as P


F32 = jnp.float32
BF16 = jnp.bfloat16
FULL = 8
PART = 4
NO_SLOT = 99.0


def dot(left, right):
    return jnp.dot(left, right, preferred_element_type=F32)


def contract_rows(left, right):
    return lax.dot_general(left, right, (((1,), (1,)), ((), ())), preferred_element_type=F32)


def contract_cols(left, right):
    return lax.dot_general(left, right, (((0,), (0,)), ((), ())), preferred_element_type=F32)


def iota(shape, dim):
    return lax.broadcasted_iota(jnp.int32, shape, dim)


def dispatch_body(experts, parts, ids_hbm, gates_hbm, tokens_hbm, grad_hbm, first_hbm, second_hbm, *scratch):
    ids_ref, gates_ref, both_ref, first_ref, second_ref, in_sems, out_sems = scratch
    rows = tokens_hbm.shape[0]
    early = [
        pltpu.make_async_copy(ids_hbm, ids_ref, in_sems.at[0]),
        pltpu.make_async_copy(gates_hbm, gates_ref, in_sems.at[1]),
    ]
    late = [
        pltpu.make_async_copy(tokens_hbm, both_ref.at[pl.ds(0, rows)], in_sems.at[2]),
        pltpu.make_async_copy(grad_hbm, both_ref.at[pl.ds(rows, rows)], in_sems.at[3]),
    ]
    for copy in early + late:
        copy.start()
    for copy in early:
        copy.wait()
    expert = iota((experts, rows), 0)
    member = jnp.zeros((experts, rows), F32)
    gate = jnp.zeros((experts, rows), F32)
    for k in range(ids_ref.shape[0]):
        hit = ids_ref[k : k + 1, :] == expert
        member = jnp.where(hit, 1.0, member)
        gate = jnp.where(hit, gates_ref[k : k + 1, :], gate)
    earlier = jnp.where(iota((rows, rows), 0) < iota((rows, rows), 1), 1.0, 0.0).astype(BF16)
    rank = jnp.where(member > 0.5, dot(member.astype(BF16), earlier), NO_SLOT)

    def picks(depth, base, low, high):
        shape = (high - low, 2 * depth, rows)
        flat = ((high - low) * 2 * depth, rows)
        row = iota(shape, 1)
        slot = (jnp.where(row < depth, row, row - depth) + base).astype(F32)
        is_token = row < depth
        hit = rank[low:high, None, :] == slot
        one = jnp.where(hit, 1.0, 0.0)
        of_token = jnp.where(is_token, one, 0.0).reshape(flat)
        of_grad = jnp.where(is_token, 0.0, one).reshape(flat)
        scale = jnp.where(hit, jnp.broadcast_to(gate[low:high, None, :], shape), 0.0)
        scale = jnp.sum(jnp.where(is_token, one, scale).reshape(flat), axis=1, keepdims=True)
        return jnp.concatenate([of_token, of_grad], axis=1).astype(BF16), scale

    per = experts // parts
    stores = []
    for p in range(parts):
        for depth, base, buf, out in ((FULL, 0, first_ref, first_hbm), (PART, FULL, second_ref, second_hbm)):
            pick, scale = picks(depth, base, p * per, (p + 1) * per)
            if not stores:
                for copy in late:
                    copy.wait()
            span = pl.ds(p * per * 2 * depth, per * 2 * depth)
            buf[span] = (dot(pick, both_ref[...]) * scale).astype(BF16)
            stores.append(pltpu.make_async_copy(buf.at[span], out.at[span], out_sems.at[len(stores)]))
            stores[-1].start()
    for store in stores:
        store.wait()


def dispatch(ids_t, gates_t, tokens, out_grad, experts, parts):
    rows, width = tokens.shape
    shapes = [(experts * 2 * FULL, width), (experts * 2 * PART, width)]
    anywhere = pl.BlockSpec(memory_space=pl.ANY)
    return pl.pallas_call(
        lambda *refs: dispatch_body(experts, parts, *refs),
        in_specs=[anywhere] * 4,
        out_specs=[anywhere] * 2,
        out_shape=[jax.ShapeDtypeStruct(shape, BF16) for shape in shapes],
        scratch_shapes=[
            pltpu.VMEM(ids_t.shape, ids_t.dtype),
            pltpu.VMEM(gates_t.shape, gates_t.dtype),
            pltpu.VMEM((2 * rows, width), BF16),
        ]
        + [pltpu.VMEM(shape, BF16) for shape in shapes]
        + [pltpu.SemaphoreType.DMA((4,)), pltpu.SemaphoreType.DMA((2 * parts,))],
        name="dispatch",
    )(ids_t, gates_t, tokens, out_grad)


def picker_body(experts, ids_ref, gates_ref, full_ref, part_ref):
    rows, top = ids_ref.shape
    expert = iota((rows, experts), 1)
    member = jnp.zeros((rows, experts), F32)
    gate = jnp.zeros((rows, experts), F32)
    for k in range(top):
        hit = ids_ref[:, k : k + 1] == expert
        member = jnp.where(hit, 1.0, member)
        gate = jnp.where(hit, gates_ref[:, k : k + 1], gate)
    later = jnp.where(iota((rows, rows), 1) < iota((rows, rows), 0), 1.0, 0.0).astype(BF16)
    rank = jnp.where(member > 0.5, dot(later, member.astype(BF16)), NO_SLOT).astype(BF16)
    high = gate.astype(BF16)
    low = (gate - high.astype(F32)).astype(BF16)

    def fill(out_ref, depth, base):
        total = experts * 2 * depth
        spread = jnp.where(iota((experts, total), 1) // (2 * depth) == iota((experts, total), 0), 1.0, 0.0).astype(BF16)
        place = iota((rows, total), 1) % (2 * depth)
        slot = jnp.where(place < depth, place, place - depth) + base
        hit = dot(rank, spread) == slot.astype(F32)
        back = hit & (place < depth)
        out_ref[0:rows, :] = jnp.where(back, dot(high, spread), 0.0).astype(BF16)
        out_ref[rows : 2 * rows, :] = jnp.where(back, dot(low, spread), 0.0).astype(BF16)
        out_ref[2 * rows : 3 * rows, :] = jnp.where(hit & (place >= depth), 1.0, 0.0).astype(BF16)

    fill(full_ref, FULL, 0)
    fill(part_ref, PART, FULL)


def picker(ids, gates, experts):
    rows = ids.shape[0]
    return pl.pallas_call(
        lambda *refs: picker_body(experts, *refs),
        out_shape=[
            jax.ShapeDtypeStruct((3 * rows, experts * 2 * FULL), BF16),
            jax.ShapeDtypeStruct((3 * rows, experts * 2 * PART), BF16),
        ],
        name="picker",
    )(ids, gates)


def gather_body(pick_ref, back_ref, mixed_ref, grad_ref):
    rows = mixed_ref.shape[0]
    total = dot(pick_ref[...], back_ref[...])
    mixed_ref[...] = total[0:rows] + total[rows : 2 * rows]
    grad_ref[...] = total[2 * rows : 3 * rows]


def finish_body(parts, pick_ref, back_ref, mixed_old_ref, grad_old_hbm, mixed_hbm, grad_hbm, *scratch):
    grad_old_ref, mixed_ref, grad_ref, sem, sems = scratch
    load = pltpu.make_async_copy(grad_old_hbm, grad_old_ref, sem)
    load.start()
    rows, width = mixed_ref.shape
    stores = []
    cols = width // parts
    for p in range(parts):
        low, high = p * cols, (p + 1) * cols
        total = dot(pick_ref[...], back_ref[:, low:high])
        mixed = mixed_old_ref[:, low:high] + total[0:rows] + total[rows : 2 * rows]
        mixed_ref[:, low:high] = mixed.astype(BF16)
        if not stores:
            load.wait()
        grad_ref[:, low:high] = (grad_old_ref[:, low:high] + total[2 * rows : 3 * rows]).astype(BF16)
        for ref, out in ((mixed_ref, mixed_hbm), (grad_ref, grad_hbm)):
            span = pl.ds(low, cols)
            stores.append(pltpu.make_async_copy(ref.at[:, span], out.at[:, span], sems.at[len(stores)]))
            stores[-1].start()
    for store in stores:
        store.wait()


def gather(pick, back):
    shape = (pick.shape[0] // 3, back.shape[1])
    vmem = pl.BlockSpec(memory_space=pltpu.VMEM)
    return pl.pallas_call(
        gather_body,
        in_specs=[vmem] * 2,
        out_specs=[vmem] * 2,
        out_shape=[pltpu.VMEM(shape, F32), jax.ShapeDtypeStruct(shape, F32)],
        compiler_params=pltpu.CompilerParams(vmem_limit_bytes=40 << 20),
        name="gather",
    )(pick, back)


def finish(pick, back, old, parts):
    shape = old[0].shape
    anywhere = pl.BlockSpec(memory_space=pl.ANY)
    return pl.pallas_call(
        lambda *refs: finish_body(parts, *refs),
        in_specs=[pl.BlockSpec(memory_space=pltpu.VMEM)] * 3 + [pl.BlockSpec(memory_space=pltpu.HBM)],
        out_specs=[anywhere] * 2,
        out_shape=[jax.ShapeDtypeStruct(shape, BF16)] * 2,
        scratch_shapes=[pltpu.VMEM(shape, F32)]
        + [pltpu.VMEM(shape, BF16)] * 2
        + [pltpu.SemaphoreType.DMA(()), pltpu.SemaphoreType.DMA((2 * parts,))],
        compiler_params=pltpu.CompilerParams(vmem_limit_bytes=24 << 20),
        name="finish",
    )(in_vmem(pick), in_vmem(back), in_vmem(old[0]), in_hbm(old[1]))


def in_hbm(array):
    return pltpu.with_memory_space_constraint(array, pltpu.HBM)


def in_vmem(array):
    return pltpu.with_memory_space_constraint(array, pltpu.VMEM)


def expert_rows(x, cot, wg_ref, wu_ref, wd_ref):
    pre_gate = dot(x, wg_ref[...])
    pre_up = dot(x, wu_ref[...])
    sig = jax.nn.sigmoid(pre_gate)
    hidden = (pre_gate * sig * pre_up).astype(BF16)
    result = dot(hidden, wd_ref[...]).astype(BF16)
    d_hidden = contract_rows(cot, wd_ref[...])
    d_gate = (d_hidden * pre_up * sig * (1.0 + pre_gate * (1.0 - sig))).astype(BF16)
    d_up = (d_hidden * pre_gate * sig).astype(BF16)
    d_rows = (contract_rows(d_gate, wg_ref[...]) + contract_rows(d_up, wu_ref[...])).astype(BF16)
    return hidden, result, d_gate, d_up, d_rows


def main_body(tok_ref, cot_ref, wg_ref, wu_ref, wd_ref, back_ref, hid_ref, dg_ref, du_ref):
    group, depth, width = tok_ref.shape
    flat = (group * depth, width)
    hidden, result, d_gate, d_up, d_rows = expert_rows(
        tok_ref[...].reshape(flat), cot_ref[...].reshape(flat), wg_ref, wu_ref, wd_ref
    )
    hid_ref[...] = hidden
    dg_ref[...] = d_gate
    du_ref[...] = d_up
    back_ref[:, 0:depth] = result.reshape(group, depth, width)
    back_ref[:, depth : 2 * depth] = d_rows.reshape(group, depth, width)


def main_experts(first, wg, wu, wd, group):
    sources, both, width = first.shape
    hidden_width = wg.shape[1]
    small = jax.ShapeDtypeStruct((sources * FULL, hidden_width), BF16)
    fixed = lambda w: pl.BlockSpec(w.shape, lambda i: (0, 0), pipeline_mode=pl.Buffered(1))
    return pl.pallas_call(
        main_body,
        grid=(sources // group,),
        in_specs=[
            pl.BlockSpec((group, FULL, width), lambda i: (i, 0, 0)),
            pl.BlockSpec((group, FULL, width), lambda i: (i, 1, 0)),
            fixed(wg),
            fixed(wu),
            fixed(wd),
        ],
        out_specs=[pl.BlockSpec((group, both, width), lambda i: (i, 0, 0))]
        + [pl.BlockSpec((group * FULL, hidden_width), lambda i: (i, 0))] * 3,
        out_shape=[jax.ShapeDtypeStruct(first.shape, BF16), small, small, small],
        name="experts_main",
    )(first, first, wg, wu, wd)


def rest_body(mix_ref, wg_ref, wu_ref, wd_ref, back_ref, tok_ref, cot_ref, hid_ref, dg_ref, du_ref):
    sources, depth, width = mix_ref.shape
    block = 256
    half = block // 2
    row = iota((block, block), 0)
    col = iota((block, block), 1)
    local = jnp.where(row < half, row, row - half)
    start = (local // PART) * (2 * PART) + local % PART + jnp.where(row < half, 0, PART)
    apart = jnp.where(col == start, 1.0, 0.0).astype(BF16)
    mix = mix_ref[...].reshape(sources * depth, width)
    n_blocks = sources * depth // block
    toks, cots = [], []
    for b in range(n_blocks):
        parts = dot(apart, mix[b * block : (b + 1) * block]).astype(BF16)
        toks.append(parts[:half])
        cots.append(parts[half:])
    tok = jnp.concatenate(toks, axis=0)
    cot = jnp.concatenate(cots, axis=0)
    hidden, result, d_gate, d_up, d_rows = expert_rows(tok, cot, wg_ref, wu_ref, wd_ref)
    per = block // depth
    for b in range(n_blocks):
        both = jnp.concatenate([result[b * half : (b + 1) * half], d_rows[b * half : (b + 1) * half]], axis=0)
        back_ref[b * per : (b + 1) * per] = contract_cols(apart, both).astype(BF16).reshape(per, depth, width)
    tok_ref[...] = tok
    cot_ref[...] = cot
    hid_ref[...] = hidden
    dg_ref[...] = d_gate
    du_ref[...] = d_up


def rest_experts(second, wg, wu, wd):
    sources, _, width = second.shape
    rows = sources * PART
    wide = jax.ShapeDtypeStruct((rows, width), BF16)
    small = jax.ShapeDtypeStruct((rows, wg.shape[1]), BF16)
    return pl.pallas_call(
        rest_body,
        in_specs=[pl.BlockSpec(memory_space=pltpu.VMEM)] * 4,
        out_shape=[jax.ShapeDtypeStruct(second.shape, BF16), wide, wide, small, small, small],
        compiler_params=pltpu.CompilerParams(vmem_limit_bytes=48 << 20),
        name="experts_rest",
    )(in_vmem(second), wg, wu, wd)


def exchange(blocks):
    return lax.all_to_all(blocks, "expert", split_axis=0, concat_axis=0, tiled=True)


def replica_sum(part):
    other = lax.ppermute(part, "dp", [(0, 1), (1, 0)])
    return (part.astype(F32) + other.astype(F32)).astype(BF16)


def layer(tokens, expert_ids, gate_weights, w_gate, w_up, w_down, out_grad):
    experts = lax.axis_size("expert")
    _, width = tokens.shape
    wg, wu, wd = w_gate[0], w_up[0], w_down[0]
    first, second = dispatch(expert_ids.T, gate_weights.T, tokens, out_grad, experts, 4)
    first = exchange(first.reshape(experts, 2 * FULL, width))
    first, second = lax.optimization_barrier((first, second))
    second = exchange(second.reshape(experts, 2 * PART, width))
    pick_full, pick_part = picker(expert_ids, gate_weights, experts)
    full, hid_a, dg_a, du_a = main_experts(first, wg, wu, wd, 32)
    part, tok_b, cot_b, hid_b, dg_b, du_b = rest_experts(second, wg, wu, wd)
    full = exchange(full)
    tok = jnp.concatenate([first[:, :FULL].reshape(-1, width), tok_b], axis=0)
    cot = jnp.concatenate([first[:, FULL:].reshape(-1, width), cot_b], axis=0)
    hid = jnp.concatenate([hid_a, hid_b], axis=0)
    d_gate = jnp.concatenate([dg_a, dg_b], axis=0)
    d_up = jnp.concatenate([du_a, du_b], axis=0)
    grad_gate = replica_sum(contract_cols(tok, d_gate).astype(BF16))
    grad_up = replica_sum(contract_cols(tok, d_up).astype(BF16))
    grad_down = replica_sum(contract_cols(hid, cot).astype(BF16))
    full, part, pick_full, pick_part, grad_gate, grad_up = lax.optimization_barrier(
        (full, part, pick_full, pick_part, grad_gate, grad_up)
    )
    full = full.reshape(-1, width)
    part = exchange(part).reshape(-1, width)
    full, grad_down = lax.optimization_barrier((full, grad_down))
    old = gather(pick_full, full)
    mixed, grad_tokens = finish(pick_part, part, old, 2)
    return mixed, grad_tokens, grad_gate[None], grad_up[None], grad_down[None]


def solution(mesh):
    by_row = P(("dp", "expert"), None)
    by_expert = P("expert", None, None)
    return jax.shard_map(
        layer,
        mesh=mesh,
        in_specs=(by_row, by_row, by_row, by_expert, by_expert, by_expert, by_row),
        out_specs=(by_row, by_row, by_expert, by_expert, by_expert),
        check_vma=False,
    )
```
